256 devices in a mesh: view: 64 (over x, z, y_lo), slab: 4 (over y_hi, core).
Axes of the slice: x: 4, y: 4 (y_hi: 2, y_lo: 2; y = y_hi * 2 + y_lo), z: 8, core: 2. Of those that a mesh axis runs over, the one named last changes fastest.
Arguments:
- target_latents: bfloat16 [64, 128, 12, 640], P('view', 'slab'), may hold values from -6 to 6
- ref_latents: bfloat16 [64, 128, 12, 640], P('view', 'slab'), may hold values from -6 to 6
- assignment: int32 [64], replicated, may hold values from 0 to 63, each once
- timestep: int32 [1], replicated, may hold values from 0 to 999
- conv_gain: float32 [640], replicated, may hold values from 0.1 to 1.9
- conv_weight: bfloat16 [3, 3, 640, 640], replicated, may hold values from -0.078125 to 0.078125
- time_weight: bfloat16 [160, 640], replicated, may hold values from -0.5 to 0.5
- attn_gain: float32 [640], replicated, may hold values from 0.1 to 1.9
- w_qkv: bfloat16 [3, 640, 640], replicated, may hold values from -12 to 12
- w_out: bfloat16 [640, 640], replicated, may hold values from -0.25 to 0.25
- mlp_gain: float32 [640], replicated, may hold values from 0.1 to 1.9
- w_up: bfloat16 [640, 2560], P(None, 'slab'), may hold values from -0.25 to 0.25
- w_down: bfloat16 [2560, 640], P('slab'), may hold values from -0.125 to 0.125
Outputs:
- section_out: bfloat16 [64, 128, 12, 640], P('view', 'slab')
The draws below stay inside these ranges and needn't reach their ends.
All inputs are finite; a program needn't handle non-finite values.
Results may differ from the reference program's by a relative error of at most 0.023.
Values may be sent and summed in bfloat16 or wider, within the bound.
No kernel may reach another device: no remote copies, remote signals or barrier semaphores. Data moves between devices by JAX's collectives and lax.ppermute only.
A program may use at most 128 MiB of HBM per device.

```python
import math
import jax
import jax.numpy as jnp
from jax import lax

C = 640
FF = 2560
HEAD_DIM = 64
HEADS = 10
TEMB = 160
COLS = 12
ROWS = 128
VIEWS = 64
REFS = 64


def draw_w_qkv(key, part):
    base = jax.random.normal(jax.random.fold_in(key, 1), (3, C, C), jnp.float32) * C ** (-0.5)
    return jnp.clip(base, -12.0, 12.0).astype(jnp.bfloat16)


def shard_levels(key, dims, split, low, top_value):
    loudness = 1.0
    for dim, blocks in split:
        draws = jax.random.uniform(jax.random.fold_in(jax.random.fold_in(key, 6), dim), (blocks,), jnp.float32, low / len(split), top_value / len(split))
        loudness = loudness * jnp.repeat(jnp.exp(draws), dims[dim] // blocks).reshape((-1,) + (1,) * (len(dims) - 1 - dim))
    return loudness


def bell_draw(own_key, dims, scale, bound, shards=(), kind=jnp.bfloat16):
    values = jax.random.normal(own_key, dims, jnp.float32) * scale
    if len(shards) > 0:
        values = shard_levels(own_key, dims, shards, -0.22, 0.18) * values
    return jnp.clip(values, min=-bound, max=bound).astype(kind)


def setup_inputs(seed: int = 0) -> dict:
    splits = jax.random.split(jax.random.key(seed), 14)
    return {
        "target_latents": bell_draw(splits[0], (VIEWS, ROWS, COLS, C), 1.0, 6.0, ((0, 64), (1, 4))),
        "ref_latents": bell_draw(splits[1], (REFS, ROWS, COLS, C), 1.0, 6.0, ((0, 64), (1, 4))),
        "assignment": jax.random.permutation(splits[2], VIEWS).astype(jnp.int32),
        "timestep": jax.random.randint(splits[3], (1,), 0, 1000).astype(jnp.int32),
        "conv_gain": jnp.clip(1.0 + 0.18 * jax.random.normal(splits[4], (C,), jnp.float32), 0.1, 1.9),
        "conv_weight": bell_draw(splits[5], (3, 3, C, C), (9 * C) ** -0.5, 0.078125),
        "time_weight": bell_draw(splits[6], (TEMB, C), TEMB ** -0.5, 0.5),
        "attn_gain": jnp.clip(1.0 + 0.18 * jax.random.normal(splits[7], (C,), jnp.float32), 0.1, 1.9),
        "w_qkv": draw_w_qkv(jax.random.fold_in(splits[13], 71), 0),
        "w_out": bell_draw(splits[9], (C, C), C ** -0.5, 0.25),
        "mlp_gain": jnp.clip(1.0 + 0.18 * jax.random.normal(splits[10], (C,), jnp.float32), 0.1, 1.9),
        "w_up": bell_draw(splits[11], (C, FF), C ** -0.5, 0.25, ((1, 4),)),
        "w_down": bell_draw(splits[12], (FF, C), FF ** -0.5, 0.125, ((0, 4),)),
    }


def layer_norm(values, gain_vec):
    center = values - lax.optimization_barrier(jnp.mean(values, axis=-1, keepdims=True))
    spread = lax.optimization_barrier(jnp.mean(center * center, axis=-1, keepdims=True))
    return center * lax.rsqrt(spread + 1e-05) * gain_vec

def time_embed(timestep, time_weight):
    half_dim = TEMB // 2
    frequency = jnp.exp(-math.log(10000.0) * jnp.arange(half_dim, dtype=jnp.float32) / half_dim)
    phases = timestep.astype(jnp.float32)[0] * frequency
    features = jax.nn.silu(jnp.concatenate([jnp.cos(phases), jnp.sin(phases)])).astype(jnp.bfloat16)
    return jnp.dot(features[None, :], time_weight, preferred_element_type=jnp.float32)[0]

def conv_field(active, conv_weight):
    row_count, col_count = (active.shape[0], active.shape[1])
    padded = jnp.pad(active, ((1, 1), (1, 1), (0, 0))).astype(jnp.float32)
    kernel = conv_weight.astype(jnp.float32)
    summed = jnp.zeros((row_count, col_count, kernel.shape[3]), jnp.float32)
    for row_off in range(3):
        for col_off in range(3):
            window = padded[row_off:row_off + row_count, col_off:col_off + col_count]
            summed = summed + jnp.einsum('hwc,cd->hwd', window, kernel[row_off, col_off])
    return summed

def section(latent, conv_gain, conv_weight, time_shift):
    widened = latent.astype(jnp.float32)
    active = jax.nn.silu(layer_norm(widened, conv_gain)).astype(jnp.bfloat16)
    return (widened + conv_field(active, conv_weight) + time_shift).astype(jnp.bfloat16)

def row_attend(operands):
    queries, key_rows, value_rows, ref_keys, ref_values = operands
    view_count, col_count = (queries.shape[0], queries.shape[1])
    score_scale = HEAD_DIM ** (-0.5)
    flat_shape = (view_count * col_count, HEADS, HEAD_DIM)
    flat_q = queries.reshape(flat_shape).astype(jnp.float32)
    flat_k = key_rows.reshape(flat_shape).astype(jnp.float32)
    flat_v = value_rows.reshape(flat_shape).astype(jnp.float32)
    scores = jnp.einsum('qhd,khd->hqk', flat_q, flat_k) * score_scale
    weights = jax.nn.softmax(scores, axis=-1).astype(jnp.bfloat16)
    joint_out = jnp.einsum('hqk,khd->qhd', weights.astype(jnp.float32), flat_v).reshape(view_count, col_count, HEADS * HEAD_DIM)
    view_shape = (view_count, col_count, HEADS, HEAD_DIM)
    view_q = queries.reshape(view_shape).astype(jnp.float32)
    view_k = ref_keys.reshape(view_shape).astype(jnp.float32)
    view_v = ref_values.reshape(view_shape).astype(jnp.float32)
    ref_scores = jnp.einsum('vqhd,vkhd->vhqk', view_q, view_k) * score_scale
    ref_weights = jax.nn.softmax(ref_scores, axis=-1).astype(jnp.bfloat16)
    ref_out = jnp.einsum('vhqk,vkhd->vqhd', ref_weights.astype(jnp.float32), view_v).reshape(view_count, col_count, HEADS * HEAD_DIM)
    return (joint_out + ref_out).astype(jnp.bfloat16)

def reference(target_latents, ref_latents, assignment, timestep, conv_gain, conv_weight, time_weight, attn_gain, w_qkv, w_out, mlp_gain, w_up, w_down):
    time_shift = time_embed(timestep, time_weight)

    def run_section(latent):
        return section(latent, conv_gain, conv_weight, time_shift)
    target_state = lax.map(run_section, target_latents)
    ref_state = lax.map(run_section, ref_latents)
    target_normed = layer_norm(target_state.astype(jnp.float32), attn_gain).astype(jnp.bfloat16).astype(jnp.float32)
    ref_normed = layer_norm(ref_state.astype(jnp.float32), attn_gain).astype(jnp.bfloat16).astype(jnp.float32)

    def apply_matrix(normed, matrix):
        return jnp.einsum('vrwc,cd->vrwd', normed, matrix.astype(jnp.float32)).astype(jnp.bfloat16)
    queries = apply_matrix(target_normed, w_qkv[0])
    key_rows = apply_matrix(target_normed, w_qkv[1])
    value_rows = apply_matrix(target_normed, w_qkv[2])
    ref_keys = apply_matrix(ref_normed, w_qkv[1])[assignment]
    ref_values = apply_matrix(ref_normed, w_qkv[2])[assignment]

    def by_rows(array):
        return jnp.transpose(array, (1, 0, 2, 3))
    attended = lax.map(row_attend, (by_rows(queries), by_rows(key_rows), by_rows(value_rows), by_rows(ref_keys), by_rows(ref_values)))
    attended = by_rows(attended)
    updated = (target_state.astype(jnp.float32) + jnp.einsum('vrwc,cd->vrwd', attended.astype(jnp.float32), w_out.astype(jnp.float32))).astype(jnp.bfloat16)

    def feed_forward(view_block):
        widened = view_block.astype(jnp.float32)
        normed = layer_norm(widened, mlp_gain).astype(jnp.bfloat16)
        hidden = jax.nn.gelu(jnp.einsum('rwc,cf->rwf', normed.astype(jnp.float32), w_up.astype(jnp.float32))).astype(jnp.bfloat16)
        return (widened + jnp.einsum('rwf,fc->rwc', hidden.astype(jnp.float32), w_down.astype(jnp.float32))).astype(jnp.bfloat16)
    return lax.map(feed_forward, updated)
```

```python
import math

import jax
import jax.numpy as jnp
import numpy as np
from jax import lax
from jax.experimental import pallas as pl
from jax.experimental.pallas import tpu as pltpu
from jax.sharding import Mesh, PartitionSpec as P

HEAD_DIM = 64
C = 640
ROWS = 32
COLS = 12
PAD = 16
TOK = ROWS * COLS
PTOK = ROWS * PAD
BF = jnp.bfloat16
F32 = jnp.float32
VMEM = pl.BlockSpec(memory_space=pltpu.VMEM)
ANY = pl.BlockSpec(memory_space=pl.ANY)


def dot(a, b):
    return lax.dot_general(a, b, (((1,), (0,)), ((), ())), preferred_element_type=F32)


def dot_t(a, b):
    return lax.dot_general(a, b, (((1,), (1,)), ((), ())), preferred_element_type=F32)


def norm_rows(x, gain):
    center = x - jnp.mean(x, axis=-1, keepdims=True)
    spread = jnp.mean(center * center, axis=-1, keepdims=True)
    return center * lax.rsqrt(spread + 1e-05) * gain


def time_embed(timestep, time_weight):
    half_dim = time_weight.shape[0] // 2
    frequency = jnp.exp(-math.log(10000.0) * jnp.arange(half_dim, dtype=F32) / half_dim)
    phases = timestep.astype(F32)[0] * frequency
    features = jax.nn.silu(jnp.concatenate([jnp.cos(phases), jnp.sin(phases)])).astype(BF)
    return jnp.dot(features[None, :], time_weight, preferred_element_type=F32)


def index_tables():
    t = np.arange(TOK)
    dense = np.full((TOK, 128), -1, np.int32)
    dense[:, 0] = 16 * (t // 12) + t % 12
    dense[:, 1] = 16 * (t // 12) + 12 + (t % 12) % 4
    dense[:, 2] = (t % 12) // 4
    q = np.arange(PTOK)
    padded = np.full((PTOK, 128), -10000, np.int32)
    padded[:, 0] = np.where(q % 16 < 12, 12 * (q // 16) + q % 16, -10000)
    padded[:, 1] = np.where(q % 16 >= 12, 12 * (q // 16) + q % 16 - 12, -10000)
    return dense, padded


def one_hot(column, width):
    lanes = lax.broadcasted_iota(jnp.int32, (column.shape[0], width), 1)
    return jnp.where(lanes == column, 1.0, 0.0).astype(BF)


def decode(chunks, tab):
    body = dot(one_hot(tab[:, 0:1], PTOK), chunks).astype(BF)
    rest = dot(one_hot(tab[:, 1:2], PTOK), chunks[:, :384])
    which = tab[:, 2:3]
    last = jnp.where(which == 0, rest[:, :128], jnp.where(which == 1, rest[:, 128:256], rest[:, 256:]))
    return jnp.concatenate([body, last.astype(BF)], axis=1)


def front_kernel(lat, before, after, gain, w_hbm, shift, attn_gain, state, chunk, act, cols, w, acc, sem):
    copies = [pltpu.make_async_copy(w_hbm.at[i], w.at[i], sem.at[i]) for i in range(3)]
    for copy in copies:
        copy.start()
    act[...] = jnp.zeros_like(act)
    g = gain[...].reshape(1, 1, C)

    def activate(x):
        y = norm_rows(x.astype(F32), g)
        return y * jax.nn.sigmoid(y)

    act[0:1, 0:COLS, :] = activate(before[...])
    act[ROWS + 1 : ROWS + 2, 0:COLS, :] = activate(after[...])

    def fill(i, _):
        act[pl.ds(1 + 4 * i, 4), 0:COLS, :] = activate(lat[pl.ds(4 * i, 4)])
        return 0

    lax.fori_loop(0, ROWS // 4, fill, 0)
    span = (ROWS + 2) * PAD
    for k in range(5):
        lanes = slice(128 * k, 128 * k + 128)
        a = act[:, :, lanes].reshape(span, 128)
        for j, turned in enumerate((pltpu.roll(a, 1, 0), a, pltpu.roll(a, span - 1, 0))):
            cols[:, j * C + 128 * k : j * C + 128 * k + 128] = turned.astype(BF)
    for i in range(3):
        copies[i].wait()
        part = dot(cols[i * PAD : i * PAD + PTOK, :], w[i])
        acc[...] = part if i == 0 else acc[...] + part
    ts = shift[...].reshape(1, 1, C)
    ag = attn_gain[...].reshape(1, 1, C)
    row = lax.broadcasted_iota(jnp.int32, (4 * PAD, 128), 0) % PAD
    low = row >= COLS

    def finish(i, _):
        summed = acc[pl.ds(pl.multiple_of(64 * i, 64), 64), :].reshape(4, PAD, C)[:, :COLS]
        st = (lat[pl.ds(4 * i, 4)].astype(F32) + summed + ts).astype(BF).astype(F32)
        act[pl.ds(4 * i, 4), 0:COLS, :] = st
        state[pl.ds(4 * i, 4)] = act[pl.ds(4 * i, 4)].astype(BF)
        act[pl.ds(4 * i, 4), 0:COLS, :] = norm_rows(st, ag)
        tail = act[pl.ds(4 * i, 4), :, 512:640].reshape(4 * PAD, 128)
        for j in range(4):
            piece = act[pl.ds(4 * i, 4), :, 128 * j : 128 * j + 128].reshape(4 * PAD, 128)
            if j < 3:
                piece = jnp.where(low, pltpu.roll(tail, 12 - 4 * j, 0), piece)
            chunk[pl.ds(4 * i, 4), :, 128 * j : 128 * j + 128] = piece.astype(BF).reshape(4, PAD, 128)
        return 0

    lax.fori_loop(0, ROWS // 4, finish, 0)


def front(lat, before, after, gain, weight, shift, attn_gain):
    return pl.pallas_call(
        front_kernel,
        name="front",
        out_shape=(
            jax.ShapeDtypeStruct((ROWS, PAD, C), BF),
            jax.ShapeDtypeStruct((ROWS, PAD, 512), BF),
        ),
        in_specs=[VMEM, VMEM, VMEM, VMEM, ANY, VMEM, VMEM],
        out_specs=(VMEM, VMEM),
        scratch_shapes=[
            pltpu.VMEM((ROWS + 2, PAD, C), F32),
            pltpu.VMEM(((ROWS + 2) * PAD, 3 * C), BF),
            pltpu.VMEM((3, 3 * C, C), BF),
            pltpu.VMEM((PTOK, C), F32),
            pltpu.SemaphoreType.DMA((3,)),
        ],
        compiler_params=pltpu.CompilerParams(vmem_limit_bytes=40 << 20),
        cost_estimate=pl.CostEstimate(flops=2 * PTOK * 9 * C * C, bytes_accessed=9 << 20, transcendentals=TOK * C),
    )(lat, before, after, gain, weight, shift, attn_gain)


def decode_kernel(chunks, tab, out):
    out[...] = decode(chunks[...].reshape(PTOK, 512), tab[...])


def decode_call(chunks, tab):
    return pl.pallas_call(
        decode_kernel,
        name="decode",
        out_shape=jax.ShapeDtypeStruct((TOK, C), BF),
        in_specs=[VMEM, VMEM],
        out_specs=VMEM,
        compiler_params=pltpu.CompilerParams(vmem_limit_bytes=16 << 20),
        cost_estimate=pl.CostEstimate(flops=2 * TOK * PTOK * 900, bytes_accessed=1 << 20, transcendentals=0),
    )(chunks, tab)


def attn_kernel(own, other, ref_own, ref_other, pick, w_qkv, ptab, chunk, q, k, v, rk, rv, att, ref):
    wq, wk, wv = w_qkv[0], w_qkv[1], w_qkv[2]
    q[...] = (dot(own[...], wq) * (HEAD_DIM**-0.5)).astype(BF)
    for half, x in enumerate((own, other)):
        k[half * TOK : half * TOK + TOK, :] = dot(x[...], wk).astype(BF)
        v[half * TOK : half * TOK + TOK, :] = dot(x[...], wv).astype(BF)
    spot = pick[:, 0:1]
    ref[...] = (
        dot(one_hot(spot, TOK), ref_own[...]) + dot(one_hot(spot - TOK, TOK), ref_other[...])
    ).astype(BF)
    rk[...] = dot(ref[...], wk).astype(BF)
    rv[...] = dot(ref[...], wv).astype(BF)
    lane = lax.broadcasted_iota(jnp.int32, (TOK, 128), 1)
    blocks = 4
    width = TOK // blocks
    row = lax.broadcasted_iota(jnp.int32, (width, width), 0)
    col = lax.broadcasted_iota(jnp.int32, (width, width), 1)
    same = (row // COLS) == (col // COLS)
    ones = jnp.ones((2 * TOK, 128), BF)

    def pair(p, _):
        at = pl.ds(pl.multiple_of(128 * p, 128), 128)
        q2, k2, v2 = q[:, at], k[:, at], v[:, at]
        rk2, rv2 = rk[:, at], rv[:, at]
        v_ext = jnp.concatenate([v2, ones], axis=1)
        rv_ext = jnp.concatenate([rv2, ones[:TOK]], axis=1)
        outs = []
        for h in range(2):
            qh = jnp.where((lane < HEAD_DIM) == (h == 0), q2, jnp.zeros_like(q2))
            s = dot_t(qh, k2)
            e = jnp.exp(s - jnp.max(s, axis=-1, keepdims=True)).astype(BF)
            o = dot(e, v_ext)
            joint = o[:, :128] / o[:, 128:]
            parts = []
            for b in range(blocks):
                rows = slice(b * width, b * width + width)
                s = dot_t(qh[rows], rk2[rows])
                s = jnp.where(same, s, -jnp.inf)
                e = jnp.exp(s - jnp.max(s, axis=-1, keepdims=True)).astype(BF)
                o = dot(e, rv_ext[rows])
                parts.append(o[:, :128] / o[:, 128:])
            outs.append(joint + jnp.concatenate(parts, axis=0))
        att[:, at] = jnp.where(lane < HEAD_DIM, outs[0], outs[1]).astype(BF)
        return 0

    lax.fori_loop(0, C // 128, pair, 0)
    tab = ptab[...]
    body = dot(one_hot(tab[:, 0:1], TOK), att[:, :512])
    for j in range(4):
        piece = body[:, 128 * j : 128 * j + 128]
        if j < 3:
            piece = piece + dot(one_hot(tab[:, 1:2] + 4 * j, TOK), att[:, 512:])
        chunk[:, :, 128 * j : 128 * j + 128] = piece.astype(BF).reshape(ROWS, PAD, 128)


def attn(own, other, ref_own, ref_other, pick, w_qkv, ptab):
    return pl.pallas_call(
        attn_kernel,
        name="attn",
        out_shape=jax.ShapeDtypeStruct((ROWS, PAD, 512), BF),
        in_specs=[VMEM] * 7,
        out_specs=VMEM,
        scratch_shapes=[
            pltpu.VMEM((TOK, C), BF),
            pltpu.VMEM((2 * TOK, C), BF),
            pltpu.VMEM((2 * TOK, C), BF),
            pltpu.VMEM((TOK, C), BF),
            pltpu.VMEM((TOK, C), BF),
            pltpu.VMEM((TOK, C), BF),
            pltpu.VMEM((TOK, C), BF),
        ],
        compiler_params=pltpu.CompilerParams(vmem_limit_bytes=40 << 20),
        cost_estimate=pl.CostEstimate(flops=6 * 10**9, bytes_accessed=6 << 20, transcendentals=4 * 10**6),
    )(own, other, ref_own, ref_other, pick, w_qkv, ptab)


def tail_kernel(chunks, state, tab, ptab, w_out, gain, *refs):
    ups, downs, out = refs[:4], refs[4:8], refs[8]
    att = decode(chunks[...].reshape(PTOK, 512), tab[...])
    base = dot(one_hot(tab[:, 0:1], PTOK), state[...].reshape(PTOK, C))
    updated = (base + dot(att, w_out[...])).astype(BF).astype(F32)
    normed = norm_rows(updated, gain[...]).astype(BF)
    total = updated
    for up, down in zip(ups, downs):
        hidden = jax.nn.gelu(dot(normed, up[...])).astype(BF)
        total = total + dot(hidden, down[...])
    wide = dot(one_hot(ptab[:, 0:1], TOK), total.astype(BF)).reshape(ROWS, PAD, C)
    out[0] = wide[:, :COLS].astype(BF)


def tail(chunks, state, tab, ptab, w_out, gain, ups, downs):
    return pl.pallas_call(
        tail_kernel,
        name="tail",
        out_shape=jax.ShapeDtypeStruct((1, ROWS, COLS, C), BF),
        in_specs=[VMEM] * 14,
        out_specs=VMEM,
        compiler_params=pltpu.CompilerParams(vmem_limit_bytes=50 << 20),
        cost_estimate=pl.CostEstimate(flops=3 * 10**9, bytes_accessed=9 << 20, transcendentals=10**6),
    )(chunks, state, tab, ptab, w_out, gain, *ups, *downs)


AXES = ("x", "z", "yl", "yh", "core")


def shards(
    target_latents,
    ref_latents,
    assignment,
    timestep,
    conv_gain,
    conv_weight,
    time_weight,
    attn_gain,
    w_qkv,
    w_out,
    mlp_gain,
    w_up,
    w_down,
):
    dense_np, padded_np = index_tables()
    tab, ptab = jnp.asarray(dense_np), jnp.asarray(padded_np)
    target, ref = target_latents[0], ref_latents[0]
    slab = ("yh", "core")
    up = [(i, i + 1) for i in range(3)]
    down = [(i + 1, i) for i in range(3)]
    last = jnp.concatenate([target[ROWS - 1 :], ref[ROWS - 1 :]], axis=0)
    first = jnp.concatenate([target[:1], ref[:1]], axis=0)
    before = lax.ppermute(last, slab, up)
    after = lax.ppermute(first, slab, down)

    shift = time_embed(timestep, time_weight)
    gain, again, mgain = conv_gain[None], attn_gain[None], mlp_gain[None]
    weight = conv_weight.reshape(3, 3 * C, C)
    state, sent = front(target, before[:1], after[:1], gain, weight, shift, again)
    got = lax.all_to_all(sent, ("x", "z"), split_axis=0, concat_axis=0, tiled=True)
    _, ref_sent = front(ref, before[1:], after[1:], gain, weight, shift, again)
    ref_got = lax.all_to_all(ref_sent, ("x", "z"), split_axis=0, concat_axis=0, tiled=True)

    cross = [(0, 3), (3, 0), (1, 2), (2, 1)]
    swap = [(0, 1), (1, 0)]
    far_up, far_down = lax.ppermute(w_up, ("yl", "yh"), cross), lax.ppermute(w_down, ("yl", "yh"), cross)
    ups = [w_up, lax.ppermute(w_up, "core", swap), far_up, lax.ppermute(far_up, "core", swap)]
    downs = [w_down, lax.ppermute(w_down, "core", swap), far_down, lax.ppermute(far_down, "core", swap)]

    own = decode_call(got, tab)
    other = lax.ppermute(own, "yl", swap)
    ref_own = decode_call(ref_got, tab)
    ref_other = lax.ppermute(ref_own, "yl", swap)

    yl = lax.axis_index("yl")
    mine = lax.dynamic_slice_in_dim(assignment.reshape(ROWS, 2), yl, 1, axis=1)
    place = mine // 2 + jnp.where(mine % 2 == yl, 0, ROWS)
    pick = (place * COLS + jnp.arange(COLS, dtype=jnp.int32)[None, :]).reshape(TOK, 1)
    pick = jnp.broadcast_to(pick, (TOK, 128))

    attended = attn(own, other, ref_own, ref_other, pick, w_qkv, ptab)
    back = lax.all_to_all(attended, ("x", "z"), split_axis=0, concat_axis=0, tiled=True)
    return tail(back, state, tab, ptab, w_out, mgain, ups, downs)


def solution(mesh):
    split = Mesh(mesh.devices.reshape(4, 8, 2, 2, 2), AXES)
    view, slab = ("x", "z", "yl"), ("yh", "core")
    return jax.shard_map(
        shards,
        mesh=split,
        in_specs=(
            P(view, slab, None, None),
            P(view, slab, None, None),
            P(),
            P(),
            P(),
            P(),
            P(),
            P(),
            P(),
            P(),
            P(),
            P(None, slab),
            P(slab, None),
        ),
        out_specs=P(view, slab, None, None),
        check_vma=False,
    )
```
